256 devices in a mesh: blk: 64 (over y_hi, x, z), team: 4 (over y_lo, core).
Axes of the slice: x: 4, y: 4 (y_hi: 2, y_lo: 2; y = y_hi * 2 + y_lo), z: 8, core: 2. Of those that a mesh axis runs over, the one named last changes fastest.
Arguments:
- points: float32 [16384, 1024], P('blk'), may hold values from -80 to 80
- probes: float32 [16384, 256], P('blk'), may hold values from -6 to 6
Outputs:
- product: float32 [16384, 256], P(('blk', 'team'))
The draws below stay inside these ranges and needn't reach their ends.
All inputs are finite; a program needn't handle non-finite values.
Results may differ from the reference program's by a relative error of at most 0.00014.
Values sent between devices are 32-bit elements; how exact they have to be, the bound alone decides.
No kernel may reach another device: no remote copies, remote signals or barrier semaphores. Data moves between devices by JAX's collectives and lax.ppermute only.
A program may use at most 64 MiB of HBM per device.

```python
import jax
import jax.numpy as jnp
from jax import lax

D = 1024
R = 256
LATENT = 16
ROWS = 256
POINTS = 16384
N_BLK = 64


def draw_points(key, part):
    first = jax.random.fold_in(key, 11)
    second = jax.random.fold_in(key, 23)
    third = jax.random.fold_in(key, 37)
    latent = jnp.clip(jax.random.normal(first, (POINTS, LATENT), jnp.float32), -4.0, 4.0)
    mixing = jnp.clip(jax.random.normal(second, (LATENT, D), jnp.float32), -4.0, 4.0) / 4.0
    noise = jnp.clip(jax.random.normal(third, (POINTS, D), jnp.float32), -4.0, 4.0) * 0.3
    return jnp.dot(latent, mixing) + noise


def block_scale(own_key, dims, shards, smallest, high):
    gain, own = 1.0, jax.random.fold_in(own_key, 6)
    for axis_at, parts in shards:
        steps = jnp.exp(jax.random.uniform(jax.random.fold_in(own, axis_at), (parts,), jnp.float32, smallest / len(shards), high / len(shards)))
        gain = gain * jnp.repeat(steps, dims[axis_at] // parts).reshape([-1 if axis == axis_at else 1 for axis in range(len(dims))])
    return gain


def bell_draw(own_key, extent, spread, most, pieces=(), dtype=jnp.bfloat16):
    factor_of = block_scale(own_key, extent, pieces, -0.22, 0.18) if pieces else 1.0
    drawn = jax.random.normal(own_key, extent, jnp.float32) * spread * factor_of
    return jnp.minimum(jnp.maximum(drawn, -most), most).astype(dtype)


def setup_inputs(seed: int = 0) -> dict:
    seeds = jax.random.split(jax.random.key(seed), 3)
    points = draw_points(jax.random.fold_in(seeds[2], 71), 0)
    probes = bell_draw(seeds[1], (POINTS, R), 1.0, 6.0, ((0, 64),), jnp.float32)
    return dict(points=points, probes=probes)


def reference(points, probes):
    scale = 2.0 / points.shape[1]
    sq = jnp.sum(points * points, axis=1)
    blocks = points.reshape(N_BLK, ROWS, points.shape[1])
    sq_blocks = sq.reshape(N_BLK, ROWS)

    def one_block(pair):
        rows, rows_sq = pair
        cross = lax.dot_general(rows, points, (((1,), (1,)), ((), ())), precision=lax.Precision.HIGHEST, preferred_element_type=jnp.float32)
        arg = (rows_sq[:, None] + sq[None, :] - 2.0 * cross) * scale
        kernel = jnp.exp(-jnp.maximum(arg, 0.0))
        return jnp.dot(kernel, probes, precision=lax.Precision.HIGHEST, preferred_element_type=jnp.float32)

    result = lax.map(one_block, (blocks, sq_blocks))
    return result.reshape(N_BLK * ROWS, probes.shape[1])
```

```python
import functools

import jax
import jax.numpy as jnp
from jax import lax
from jax.experimental import pallas as pl
from jax.experimental.pallas import tpu as pltpu
from jax.sharding import Mesh, PartitionSpec as P


Y, X, Z = 4, 4, 8
PLANE = ("y_hi", "x", "y_lo", "core")
ROW_TILE = 256
COL_TILE = 256


def plane_move(value, stage, step):
    def place(y, x, core):
        return ((y // 2 * X + x) * 2 + y % 2) * 2 + core

    pairs = []
    for y in range(Y):
        for x in range(X):
            for core in range(2):
                along_x = (core == 0) == (stage == 1)
                to = (y, (x + step) % X) if along_x else ((y + step) % Y, x)
                pairs.append((place(y, x, core), place(*to, core)))
    return lax.ppermute(value, PLANE, pairs)


def line_move(value):
    pairs = [
        (z * 2 + core, (z + 1 - 2 * core) % Z * 2 + core) for z in range(Z) for core in range(2)
    ]
    return lax.ppermute(value, ("z", "core"), pairs)


def core_swap(value):
    return lax.ppermute(value, "core", [(0, 1), (1, 0)])


def split2(x):
    high = x.astype(jnp.bfloat16)
    low = (x - high.astype(jnp.float32)).astype(jnp.bfloat16)
    return high, low


def split3(x):
    high = x.astype(jnp.bfloat16)
    rest = x - high.astype(jnp.float32)
    mid = rest.astype(jnp.bfloat16)
    low = (rest - mid.astype(jnp.float32)).astype(jnp.bfloat16)
    return high, mid, low


def across(a, b):
    return lax.dot_general(a, b, (((1,), (1,)), ((), ())), preferred_element_type=jnp.float32)


def product_kernel(n_rows, n_cols, scale, *refs):
    row_refs, refs = refs[:n_rows], refs[n_rows:]
    col_refs, refs = refs[:n_cols], refs[n_cols:]
    out_ref, c_high, c_mid, c_low, v_high, v_low, c_sq = refs
    width = c_high.shape[1]
    at = 0
    for ref in col_refs:
        size = ref.shape[0]
        tile = 128 if size % 128 == 0 and at % 128 == 0 else 64

        def prepare(i, _, ref=ref, at=at, tile=tile):
            here = pl.ds(pl.multiple_of(i * tile, tile), tile)
            there = pl.ds(pl.multiple_of(at + i * tile, tile), tile)
            x = ref[here, :width]
            c_high[there, :], c_mid[there, :], c_low[there, :] = split3(x)
            v_high[there, :], v_low[there, :] = split2(ref[here, width:])
            square = x * x
            part = square[:, :128]
            for lane in range(128, width, 128):
                part = part + square[:, lane : lane + 128]
            c_sq[there, :] = part
            return 0

        lax.fori_loop(0, size // tile, prepare, 0)
        at += size
    cols = at
    at = 0
    for ref in row_refs:
        size = ref.shape[0]
        tile = min(size, ROW_TILE)

        def rows(i, _, ref=ref, at=at, tile=tile):
            here = pl.ds(pl.multiple_of(i * tile, tile), tile)
            there = pl.ds(pl.multiple_of(at + i * tile, tile), tile)
            x = ref[here, :]
            high, mid, low = split3(x)
            sq = jnp.sum(x * x, axis=1, keepdims=True)

            def columns(j, total):
                col = pl.ds(pl.multiple_of(j * COL_TILE, COL_TILE), COL_TILE)
                ch, cm, cl = c_high[col, :], c_mid[col, :], c_low[col, :]
                cross = across(high, cl) + across(low, ch) + across(mid, cm)
                cross = cross + across(high, cm) + across(mid, ch)
                cross = cross + across(high, ch)
                other = jnp.sum(c_sq[col, :].T, axis=0, keepdims=True)
                arg = (sq + other - 2.0 * cross) * scale
                kh, kl = split2(jnp.exp(-jnp.maximum(arg, 0.0)))
                vh, vl = v_high[col, :], v_low[col, :]
                more = jnp.dot(kl, vh, preferred_element_type=jnp.float32)
                more = more + jnp.dot(kh, vl, preferred_element_type=jnp.float32)
                more = more + jnp.dot(kh, vh, preferred_element_type=jnp.float32)
                return total + more

            zero = jnp.zeros((tile, out_ref.shape[1]), jnp.float32)
            out_ref[there, :] = lax.fori_loop(0, cols // COL_TILE, columns, zero)
            return 0

        lax.fori_loop(0, size // tile, rows, 0)
        at += size


def tile_product(rows, cols, scale):
    width = rows[0].shape[1]
    probes = cols[0].shape[1] - width
    r = sum(x.shape[0] for x in rows)
    c = sum(x.shape[0] for x in cols)
    vmem = pl.BlockSpec(memory_space=pltpu.VMEM)
    return pl.pallas_call(
        functools.partial(product_kernel, len(rows), len(cols), scale),
        out_shape=jax.ShapeDtypeStruct((r, probes), jnp.float32),
        in_specs=[vmem] * (len(rows) + len(cols)),
        out_specs=vmem,
        scratch_shapes=[pltpu.VMEM((c, width), jnp.bfloat16)] * 3
        + [pltpu.VMEM((c, probes), jnp.bfloat16)] * 2
        + [pltpu.VMEM((c, 128), jnp.float32)],
        cost_estimate=pl.CostEstimate(
            flops=2 * r * c * (6 * width + 3 * probes), bytes_accessed=0, transcendentals=r * c
        ),
        compiler_params=pltpu.CompilerParams(vmem_limit_bytes=40 << 20),
        name="tile_product",
    )(*rows, *cols)


def body(points, probes):
    block, width = points.shape
    scale = 2.0 / width
    core = lax.axis_index("core")
    y_lo = lax.axis_index("y_lo")
    quarter, half = block // 4, block // 2

    mine = lax.dynamic_slice_in_dim(points, (2 * y_lo + core) * quarter, quarter)
    first = [plane_move(mine, 1, step) for step in (1, -1, 2)]
    stage1 = jnp.concatenate([mine, *first])
    rows = [stage1, *(plane_move(stage1, 2, step) for step in (1, -1, 2))]

    visitor = lax.dynamic_slice_in_dim(
        jnp.concatenate([points, probes], axis=1), y_lo * half, half
    )
    cols = [visitor]
    for _ in range(3):
        cols.append(line_move(cols[-1]))
    cols.append(line_move(lax.dynamic_slice_in_dim(cols[-1], core * quarter, quarter)))
    cols.append(core_swap(jnp.concatenate(cols[1:])))

    total = tile_product(rows, cols, scale)
    for stage in (2, 1):
        part = total.reshape(4, total.shape[0] // 4, total.shape[1])
        total = part[0]
        for k, step in enumerate((-1, 1, 2)):
            total = total + plane_move(part[k + 1], stage, step)
    return total


def solution(mesh):
    axes = ("y_hi", "x", "z", "y_lo", "core")
    fine = Mesh(mesh.devices.reshape(2, X, Z, 2, 2), axes)
    in_specs = (P(("y_hi", "x", "z"), None),) * 2
    return jax.shard_map(body, mesh=fine, in_specs=in_specs, out_specs=P(axes, None), check_vma=False)
```
